32 devices in a mesh: members: 2 (over x), row: 16 (over z, y, core).
Axes of the slice: x: 2, y: 2, z: 4, core: 2. Of those that a mesh axis runs over, the one named last changes fastest.
Arguments:
- node_features: bfloat16 [32768, 512], P(('members', 'row')), parts along dimension 0, may hold values from -18 to 18
- nbr_table: int32 [128, 8], P('row'), may hold values from 0 to 27, as said below
- nbr_count: int32 [128], P('row'), may hold values from 4 to 8
- send_block: int32 [256, 1], P('row'), may hold values from 0 to 7
- w_query: bfloat16 [2, 512, 512], replicated, may hold values from -9 to 9
- w_key: bfloat16 [2, 512, 512], replicated, may hold values from -0.7 to 0.7
- w_value: bfloat16 [2, 512, 512], replicated, may hold values from -0.25 to 0.25
- w_out: bfloat16 [2, 512, 512], replicated, may hold values from -0.25 to 0.25
- w_up: bfloat16 [2, 512, 2048], replicated, may hold values from -0.25 to 0.25
- w_down: bfloat16 [2, 2048, 512], replicated, may hold values from -0.125 to 0.125
- w_virtual: bfloat16 [2, 512, 512], replicated, may hold values from -0.25 to 0.25
- gains: float32 [2, 4, 512], replicated, may hold values from 0.25 to 1.75
Outputs:
- latents_out: bfloat16 [32768, 512], P(('members', 'row')), parts along dimension 0
The draws below stay inside these ranges and needn't reach their ends.
There are 2 independent parts, one for each index of `members`. The reference program is written for one: setup_inputs(seed, part) draws one part's arguments, and reference() takes and returns one part's arrays. A program takes and returns all parts, laid end to end along the dimension named above; an argument that names none is the same for every part. Nothing has to cross between parts.
Inputs may be any that keep to these rules, and one draw needn't show every extreme that they name: `nbr_table`: entry t of a row of block g names a block of device g // 8's table: t below 12 are the device's own blocks with 2 blocks of each neighbour along the node order around them, own block b at t = 2 + b; the others are received slots as in the reference program. The first entry of each row is the block itself. Every live entry names a block that exists.
All inputs are finite; a program needn't handle non-finite values.
Results may differ from the reference program's by a relative error of at most 0.007.
Values may be sent and summed in bfloat16 or wider, within the bound.
A program may use at most 128 MiB of HBM per device.

```python
import math
import jax
import jax.numpy as jnp
from jax import lax

D = 512
FF = 2048
HEADS = 4
BLOCK = 128
NBR = 8
HALO_B = 2
SLOTS = 1
LAYERS = 2
BLK_DEV = 8
NBLK = 128
NODES = 16384
N_ROW = 16


def graph_lists(key):
    devices_count = NBLK // BLK_DEV
    near_count = 2 * HALO_B + BLK_DEV
    counts = jax.random.randint(jax.random.fold_in(key, 11), (NBLK,), NBR // 2, NBR + 1).astype(jnp.int32)
    devices = jnp.arange(devices_count, dtype=jnp.int32)
    ranking = jax.random.randint(jax.random.fold_in(key, 12), (devices_count, devices_count), 0, 1 << 20).astype(jnp.int32)
    ranking = ranking * devices_count + devices[None, :]
    ranking = jnp.where(devices[:, None] == devices[None, :], jnp.int32(1 << 30), ranking)
    order = jnp.argsort(ranking, axis=1, stable=True).astype(jnp.int32)
    most_far = min(devices_count - 1, (NBR // 2 - 1) * BLK_DEV // SLOTS)
    far_live = jax.random.randint(jax.random.fold_in(key, 13), (devices_count,), 1, most_far + 1).astype(jnp.int32)
    per_device = counts.reshape(devices_count, BLK_DEV)
    slot_number = jnp.arange(1, NBR, dtype=jnp.int32)
    live = (slot_number[None, None, :] < per_device[:, :, None]).reshape(devices_count, BLK_DEV * (NBR - 1)).astype(jnp.int32)
    rank = jnp.cumsum(live, axis=1) - 1
    far_position = (live == 1) & (rank < (far_live * SLOTS)[:, None])
    safe_rank = jnp.clip(rank, 0, devices_count * SLOTS - 1)
    peer = jnp.take_along_axis(order, jnp.clip(safe_rank // SLOTS, 0, devices_count - 1), axis=1)
    far_entry = near_count + peer * SLOTS + safe_rank % SLOTS
    lower = jnp.where(devices == 0, HALO_B, 0).astype(jnp.int32)[:, None]
    upper = jnp.where(devices == devices_count - 1, HALO_B + BLK_DEV, near_count).astype(jnp.int32)[:, None]
    random_pick = jax.random.randint(jax.random.fold_in(key, 14), (devices_count, BLK_DEV * (NBR - 1)), 0, 1 << 20).astype(jnp.int32)
    local_entry = lower + random_pick % (upper - lower)
    entries = jnp.where(far_position, far_entry, local_entry).reshape(devices_count, BLK_DEV, NBR - 1)
    own_entry = jnp.broadcast_to((HALO_B + jnp.arange(BLK_DEV, dtype=jnp.int32))[None, :, None], (devices_count, BLK_DEV, 1))
    table = jnp.concatenate((own_entry, entries), axis=2).reshape(NBLK, NBR)
    return (table.astype(jnp.int32), counts)


def draw_nbr_table(key, part):
    return graph_lists(key)[0]


def draw_nbr_count(key, part):
    return graph_lists(key)[1]


def draw_node_features(key, part):
    first, second = jax.random.split(jax.random.fold_in(key, 31), 2)
    position = jnp.arange(NODES, dtype=jnp.float32) / max(NODES - 1, 1)
    offset = jnp.clip(jax.random.normal(second, (D,), jnp.float32), -3.0, 3.0)
    ramp = jnp.exp(jnp.log(3.0) * position)
    base = jnp.clip(jax.random.normal(first, (NODES, D), jnp.float32), -6.0, 6.0)
    values = base + 0.7 * ramp[:, None] * offset[None, :]
    return values.astype(jnp.bfloat16)


def key_weights(key):
    first = jax.random.fold_in(jax.random.fold_in(key, 21), 0)
    drawn = jnp.clip(jax.random.normal(first, (LAYERS, D, D), jnp.float32), -6.0, 6.0) / jnp.sqrt(jnp.float32(D))
    return drawn


def draw_w_key(key, part):
    return key_weights(key).astype(jnp.bfloat16)


def draw_w_query(key, part):
    values = jnp.clip(jax.random.normal(jax.random.fold_in(key, 23), (LAYERS, D, D), jnp.float32), -6.0, 6.0) / jnp.sqrt(jnp.float32(D))
    return values.astype(jnp.bfloat16)


def with_ends(values, rng, low, high):
    shape = values.shape
    place = [jax.random.randint(jax.random.fold_in(rng, axis), (), 0, shape[axis]) for axis in range(len(shape))]
    values = values.at[tuple(place)].set(low)
    longest = shape.index(max(shape))
    place[longest] = (place[longest] + 1) % shape[longest]
    return values.at[tuple(place)].set(high)


def normal_values(rng, shape, deviation, limit, kind=jnp.bfloat16):
    array = deviation * jax.random.normal(rng, shape, jnp.float32)
    return jnp.clip(array, min=-limit, max=limit).astype(kind)


def setup_inputs(seed: int = 0, part: int = 0) -> dict:
    key_of = jax.random.split(jax.random.key(seed), 13)
    part_keys = jax.random.split(jax.random.fold_in(key_of[12], part), 13)
    node_features = draw_node_features(jax.random.fold_in(jax.random.fold_in(key_of[12], part), 71), part)
    nbr_table = draw_nbr_table(jax.random.fold_in(key_of[12], 71), part)
    nbr_count = draw_nbr_count(jax.random.fold_in(key_of[12], 71), part)
    send_block = with_ends(jax.random.randint(key_of[3], (N_ROW * N_ROW, SLOTS), 0, BLK_DEV), jax.random.fold_in(key_of[3], 1), 0, BLK_DEV - 1).astype(jnp.int32)
    w_query = draw_w_query(jax.random.fold_in(key_of[12], 71), part)
    w_key = draw_w_key(jax.random.fold_in(key_of[12], 71), part)
    w_value = normal_values(key_of[6], (LAYERS, D, D), D ** -0.5, 0.25)
    w_out = normal_values(key_of[7], (LAYERS, D, D), D ** -0.5, 0.25)
    w_up = normal_values(key_of[8], (LAYERS, D, FF), D ** -0.5, 0.25)
    w_down = normal_values(key_of[9], (LAYERS, FF, D), FF ** -0.5, 0.125)
    w_virtual = normal_values(key_of[10], (LAYERS, D, D), D ** -0.5, 0.25)
    gains = jnp.clip(1.0 + 0.15 * jax.random.normal(key_of[11], (LAYERS, 4, D), jnp.float32), 0.25, 1.75)
    return {"node_features": node_features, "nbr_table": nbr_table, "nbr_count": nbr_count, "send_block": send_block, "w_query": w_query, "w_key": w_key, "w_value": w_value, "w_out": w_out, "w_up": w_up, "w_down": w_down, "w_virtual": w_virtual, "gains": gains}


def normalize(values, scaling):
    centred = values - lax.optimization_barrier(jnp.mean(values, axis=-1, keepdims=True))
    spread = lax.optimization_barrier(jnp.mean(centred * centred, axis=-1, keepdims=True))
    return centred * lax.rsqrt(spread + 1e-05) * scaling

def attend(queries, table, listed, counts):
    groups, block, width = queries.shape
    slots = listed.shape[1]
    head_size = width // HEADS
    picked = table[listed]
    keys = picked[..., :width].reshape(groups, slots * block, HEADS, head_size)
    values = picked[..., width:].reshape(groups, slots * block, HEADS, head_size)
    heads_q = queries.reshape(groups, block, HEADS, head_size)
    scores = jnp.einsum('gqhd,gkhd->ghqk', heads_q.astype(jnp.float32), keys.astype(jnp.float32)) / math.sqrt(head_size)
    live = (jnp.arange(slots * block, dtype=jnp.int32) // block)[None, :] < counts[:, None]
    scores = jnp.where(live[:, None, None, :], scores, -1e+30)
    top = lax.optimization_barrier(jnp.max(scores, axis=-1, keepdims=True))
    weights = jnp.exp(scores - top)
    probs = (weights / lax.optimization_barrier(jnp.sum(weights, axis=-1, keepdims=True))).astype(jnp.bfloat16)
    context = jnp.einsum('ghqk,gkhd->gqhd', probs.astype(jnp.float32), values.astype(jnp.float32))
    return context.astype(jnp.bfloat16).reshape(groups, block, width)

def reference(node_features, nbr_table, nbr_count, send_block, w_query, w_key, w_value, w_out, w_up, w_down, w_virtual, gains):
    near_count = 2 * HALO_B + BLK_DEV
    owner = (jnp.arange(NBLK, dtype=jnp.int32) // BLK_DEV)[:, None]
    beyond = jnp.maximum(nbr_table - near_count, 0)
    peer = beyond // SLOTS
    sent = send_block[peer * N_ROW + owner, beyond % SLOTS]
    source_blocks = jnp.where(nbr_table < near_count, owner * BLK_DEV + nbr_table - HALO_B, peer * BLK_DEV + sent).astype(jnp.int32)
    latent = node_features
    for layer_index in range(LAYERS):
        current = latent.astype(jnp.float32)
        node_mean = lax.optimization_barrier(jnp.sum(current, axis=0)) / NODES
        normed = normalize(current, gains[layer_index, 0]).astype(jnp.bfloat16)
        queries = jnp.dot(normed, w_query[layer_index], preferred_element_type=jnp.float32).astype(jnp.bfloat16)
        w_pair = jnp.concatenate((w_key[layer_index], w_value[layer_index]), axis=1)
        pairs = jnp.dot(normed, w_pair, preferred_element_type=jnp.float32).astype(jnp.bfloat16).reshape(NBLK, BLOCK, 2 * D)

        def attend_device(operands):
            return attend(operands[0], pairs, operands[1], operands[2])
        context = lax.map(attend_device, (queries.reshape(N_ROW, BLK_DEV, BLOCK, D), source_blocks.reshape(N_ROW, BLK_DEV, NBR), nbr_count.reshape(N_ROW, BLK_DEV)))
        context = context.reshape(NODES, D)
        after_att = current + normalize(jnp.dot(context, w_out[layer_index], preferred_element_type=jnp.float32), gains[layer_index, 1])
        middle = normalize(after_att, gains[layer_index, 2]).astype(jnp.bfloat16)
        hidden = jax.nn.gelu(jnp.dot(middle, w_up[layer_index], preferred_element_type=jnp.float32)).astype(jnp.bfloat16)
        virtual_mean = node_mean.astype(jnp.bfloat16)
        virtual = jnp.dot(virtual_mean[None, :], w_virtual[layer_index], preferred_element_type=jnp.float32)
        output_part = normalize(jnp.dot(hidden, w_down[layer_index], preferred_element_type=jnp.float32), gains[layer_index, 3])
        latent = (after_att + output_part + virtual).astype(jnp.bfloat16)
    return latent
```

```python
import functools
import math

import jax
import jax.numpy as jnp
from jax import lax
from jax.experimental import pallas as pl
from jax.experimental.pallas import tpu as pltpu
from jax.sharding import PartitionSpec as P

HEADS = 4
HALO_B = 2
TAIL = 16
VMEM_LIMIT = 60 * 1024 * 1024


def normalize(values, scaling):
    centred = values - jnp.mean(values, axis=-1, keepdims=True)
    spread = jnp.mean(centred * centred, axis=-1, keepdims=True)
    return centred * lax.rsqrt(spread + 1e-05) * scaling


def dot(a, b):
    return jnp.dot(a, b, preferred_element_type=jnp.float32)


def gelu(x):
    return 0.5 * x * (1.0 + jnp.tanh(math.sqrt(2 / math.pi) * (x + 0.044715 * x * x * x)))


def fill_send(send_sm, normed_ref, total, send_ref, block):
    peers, slots = send_sm.shape
    width = normed_ref.shape[1]
    high = total.astype(jnp.bfloat16).astype(jnp.float32)
    line = lax.broadcasted_iota(jnp.int32, (TAIL, width), 0)
    tail = jnp.where(line == 0, high, jnp.where(line == 1, total - high, 0.0)).astype(jnp.bfloat16)

    def one(peer, carry):
        for slot in range(slots):
            own = pl.multiple_of(send_sm[peer, slot] * block, block)
            send_ref[peer, pl.ds(slot * block, block), :] = normed_ref[pl.ds(own, block), :]
        send_ref[peer, pl.ds(slots * block, TAIL), :] = tail
        return carry

    lax.fori_loop(0, peers, one, 0)


def first_kernel(block, rows, send_sm, x_ref, gains_ref, normed_ref, send_ref):
    total = jnp.zeros((1, x_ref.shape[1]), jnp.float32)
    for start in range(0, x_ref.shape[0], rows):
        x = x_ref[pl.ds(start, rows), :].astype(jnp.float32)
        total = total + jnp.sum(x, axis=0, keepdims=True)
        normed_ref[pl.ds(start, rows), :] = normalize(x, gains_ref[0, 0:1, :]).astype(jnp.bfloat16)
    fill_send(send_sm, normed_ref, total, send_ref, block)


def layer_kernel(layer, last, block, node_total, *refs):
    (table_sm, count_sm, send_sm, x_ref, normed_ref, low_ref, high_ref, far_ref, wq_ref, wk_ref, wv_ref,
     wo_ref, wu_ref, wd_ref, wm_ref, gains_ref) = refs[:16]
    if last:
        out_ref, key_ref, value_ref, context_ref, virtual_ref = refs[16:]
    else:
        out_ref, next_ref, send_ref, key_ref, value_ref, context_ref, virtual_ref, sum_ref = refs[16:]
    step = pl.program_id(0)
    rows, width = x_ref.shape
    blocks_here, slots_listed = table_sm.shape
    peers = far_ref.shape[0]
    slots = (far_ref.shape[1] - TAIL) // block
    head_size = width // HEADS
    group = rows // block
    base = low_ref.shape[0]
    own_rows = normed_ref.shape[0]

    @pl.when(step == 0)
    def _():
        def project(piece, at):
            size = piece.shape[0]
            key_ref[pl.ds(at, size), :] = dot(piece, wk_ref[...]).astype(jnp.bfloat16)
            value_ref[pl.ds(at, size), :] = dot(piece, wv_ref[...]).astype(jnp.bfloat16)

        project(low_ref[...], 0)
        project(high_ref[...], base + own_rows)
        chunk = math.gcd(own_rows, 512)

        def own_piece(i, carry):
            at = pl.multiple_of(i * chunk, chunk)
            project(normed_ref[pl.ds(at, chunk), :], pl.multiple_of(base + at, block))
            return carry

        lax.fori_loop(0, own_rows // chunk, own_piece, 0)
        many = math.gcd(peers, 4)
        span = slots * block

        def far_piece(i, carry):
            piece = far_ref[pl.ds(i * many, many), pl.ds(0, span), :].reshape(many * span, width)
            project(piece, pl.multiple_of(2 * base + own_rows + i * (many * span), block))
            return carry

        lax.fori_loop(0, peers // many, far_piece, 0)
        tails = far_ref[:, pl.ds(span, TAIL), :].astype(jnp.float32)
        node_sum = jnp.sum(jnp.sum(tails, axis=0), axis=0, keepdims=True)
        mean = jnp.broadcast_to(node_sum / node_total, (TAIL, width)).astype(jnp.bfloat16)
        virtual_ref[...] = dot(mean, wm_ref[...])

    at = pl.multiple_of(step * rows, rows)
    queries = dot(normed_ref[pl.ds(at, rows), :], wq_ref[...]).astype(jnp.bfloat16)
    scale = math.log2(math.e) / math.sqrt(head_size)
    for g in range(group):
        which = step * group + g
        count = count_sm[which]
        places = [pl.multiple_of(table_sm[which, j] * block, block) for j in range(slots_listed)]
        for h in range(HEADS):
            columns = slice(h * head_size, (h + 1) * head_size)
            q = queries[g * block : (g + 1) * block, columns]
            scores = []
            for j in range(slots_listed):
                k = key_ref[pl.ds(places[j], block), columns]
                s = lax.dot_general(q, k, (((1,), (1,)), ((), ())), preferred_element_type=jnp.float32)
                scores.append(s if j == 0 else jnp.where(j < count, s, -1e30))
            top = jnp.max(functools.reduce(jnp.maximum, scores), axis=-1, keepdims=True)
            weights = [jnp.exp2((s - top) * scale) for s in scores]
            norm = jnp.sum(functools.reduce(jnp.add, weights), axis=-1, keepdims=True)
            probs = jnp.concatenate([w.astype(jnp.bfloat16) for w in weights], axis=1)
            v = jnp.concatenate([value_ref[pl.ds(p, block), columns] for p in places], axis=0)
            context_ref[pl.ds(g * block, block), columns] = (dot(probs, v) / norm).astype(jnp.bfloat16)

    x = x_ref[...].astype(jnp.float32)
    after_att = x + normalize(dot(context_ref[...], wo_ref[...]), gains_ref[layer, 1:2, :])
    middle = normalize(after_att, gains_ref[layer, 2:3, :]).astype(jnp.bfloat16)
    hidden_size = wu_ref.shape[1]
    part = math.gcd(hidden_size, 512)
    down = None
    for f in range(0, hidden_size, part):
        hidden = gelu(dot(middle, wu_ref[:, f : f + part])).astype(jnp.bfloat16)
        term = dot(hidden, wd_ref[f : f + part, :])
        down = term if down is None else down + term
    output_part = normalize(down, gains_ref[layer, 3:4, :])
    latent = (after_att + output_part + virtual_ref[0:1, :]).astype(jnp.bfloat16)
    out_ref[...] = latent
    if not last:
        current = latent.astype(jnp.float32)
        next_ref[pl.ds(at, rows), :] = normalize(current, gains_ref[layer + 1, 0:1, :]).astype(jnp.bfloat16)
        partial = jnp.sum(current, axis=0, keepdims=True)

        @pl.when(step == 0)
        def _():
            sum_ref[0:1, :] = partial

        @pl.when(step > 0)
        def _():
            sum_ref[0:1, :] = sum_ref[0:1, :] + partial

        @pl.when(step == pl.num_programs(0) - 1)
        def _():
            fill_send(send_sm, next_ref, sum_ref[0:1, :], send_ref, block)


def fixed(shape):
    return pl.BlockSpec(shape, lambda i, *_: (0,) * len(shape), pipeline_mode=pl.Buffered(1))


def body(
    node_features,
    nbr_table,
    nbr_count,
    send_block,
    w_query,
    w_key,
    w_value,
    w_out,
    w_up,
    w_down,
    w_virtual,
    gains,
):
    blocks_here = nbr_table.shape[0]
    own_rows, width = node_features.shape
    block = own_rows // blocks_here
    peers = lax.axis_size("row")
    slots = send_block.shape[1]
    layers = w_query.shape[0]
    rows = block * math.gcd(blocks_here, 2)
    sent = jax.ShapeDtypeStruct((peers, slots * block + TAIL, width), jnp.bfloat16)
    held = jax.ShapeDtypeStruct((own_rows, width), jnp.bfloat16)
    halo = HALO_B * block
    params = pltpu.CompilerParams(vmem_limit_bytes=VMEM_LIMIT)

    normed, send = pl.pallas_call(
        functools.partial(first_kernel, block, rows),
        out_shape=(held, sent),
        grid_spec=pltpu.PrefetchScalarGridSpec(
            num_scalar_prefetch=1,
            grid=(1,),
            in_specs=[fixed(held.shape), fixed(gains.shape)],
            out_specs=[fixed(held.shape), fixed(sent.shape)],
        ),
        compiler_params=params,
        name="first",
    )(send_block, node_features, gains)

    latent = node_features
    for layer in range(layers):
        last = layer == layers - 1
        far = lax.all_to_all(send, "row", split_axis=0, concat_axis=0, tiled=True)
        low = lax.ppermute(normed[own_rows - halo :], "row", [(i, i + 1) for i in range(peers - 1)])
        high = lax.ppermute(normed[:halo], "row", [(i + 1, i) for i in range(peers - 1)])

        def of_layer(w, layer=layer):
            return pl.BlockSpec(
                (None,) + w.shape[1:], lambda i, *_: (layer, 0, 0), pipeline_mode=pl.Buffered(1)
            )

        tile = pl.BlockSpec((rows, width), lambda i, *_: (i, 0))
        table_rows = 2 * halo + own_rows + peers * slots * block
        weights = (w_query, w_key, w_value, w_out, w_up, w_down, w_virtual)
        scratch = [
            pltpu.VMEM((table_rows, width), jnp.bfloat16),
            pltpu.VMEM((table_rows, width), jnp.bfloat16),
            pltpu.VMEM((rows, width), jnp.bfloat16),
            pltpu.VMEM((TAIL, width), jnp.float32),
        ]
        result = pl.pallas_call(
            functools.partial(layer_kernel, layer, last, block, own_rows * peers),
            out_shape=(held,) if last else (held, held, sent),
            grid_spec=pltpu.PrefetchScalarGridSpec(
                num_scalar_prefetch=3,
                grid=(own_rows // rows,),
                in_specs=[tile, fixed(held.shape), fixed(low.shape), fixed(high.shape), fixed(far.shape)]
                + [of_layer(w) for w in weights]
                + [fixed(gains.shape)],
                out_specs=[tile] if last else [tile, fixed(held.shape), fixed(sent.shape)],
                scratch_shapes=scratch if last else scratch + [pltpu.VMEM((8, width), jnp.float32)],
            ),
            compiler_params=params,
            name=f"layer{layer}",
        )(nbr_table, nbr_count, send_block, latent, normed, low, high, far, *weights, gains)
        if last:
            (latent,) = result
        else:
            latent, normed, send = result
    return latent


def solution(mesh):
    in_specs = (
        P(("members", "row"), None),
        P("row", None),
        P("row"),
        P("row", None),
        P(),
        P(),
        P(),
        P(),
        P(),
        P(),
        P(),
        P(),
    )
    out_specs = P(("members", "row"), None)
    return jax.shard_map(body, mesh=mesh, in_specs=in_specs, out_specs=out_specs, check_vma=False)
```
